128 devices in a mesh: row: 16 (over x, z_hi, core), col: 8 (over y, z_lo).
Axes of the slice: x: 4, y: 4, z: 4 (z_hi: 2, z_lo: 2; z = z_hi * 2 + z_lo), core: 2. Of those that a mesh axis runs over, the one named last changes fastest.
Arguments:
- x_tiles: float32 [256, 4096], P(('row', 'col')), may hold values from -6 to 6
- ham_tiles: float32 [32768, 4096], P(('row', 'col')), may hold values from -0.0625 to 0.0625
- tile_rows: int32 [32768], P(('row', 'col')), may hold values from 0 to 15, as said below
- tile_cols: int32 [32768], P(('row', 'col')), may hold values from 0 to 31, as said below
- tile_count: int32 [128], P(('row', 'col')), may hold values from 0 to 256, as said below
Outputs:
- product: float32 [256, 4096], P(('row', 'col'))
The draws below stay inside these ranges and needn't reach their ends.
Inputs may be any that keep to these rules, and one draw needn't show every extreme that they name: For device d, its first tile_count[d] slots hold distinct positions (tile_rows, tile_cols) whose global tile row is at most the global tile column; the other slots are padding with indices in range. `tile_cols`: see tile_rows. `tile_count`: at most 256; equal to 256 on every device of row index 0.
All inputs are finite; a program needn't handle non-finite values.
Results may differ from the reference program's by a relative error of at most 0.0003.
Values sent between devices are 32-bit elements; how exact they have to be, the bound alone decides.
No kernel may reach another device: no remote copies, remote signals or barrier semaphores. Data moves between devices by JAX's collectives and lax.ppermute only.
A program may use at most 128 MiB of HBM per device.

```python
import jax
import jax.numpy as jnp
from jax import lax

TILE = 64
VECS = 64
TPD = 2
NT = 256
MAXT = 256
N_ROW = 16
N_COL = 8
DEVICES = 128


def tile_layout(key):
    rows_blk = N_COL * TPD
    cols_blk = N_ROW * TPD
    positions = rows_blk * cols_blk
    dev = jnp.arange(DEVICES, dtype=jnp.int32)
    rindex = dev // N_COL
    cindex = dev % N_COL
    spot = jnp.arange(positions, dtype=jnp.int32)
    local_a = spot // cols_blk
    local_b = spot % cols_blk
    grow = rindex[:, None] * rows_blk + local_a[None, :]
    gcol = ((local_b // TPD)[None, :] * N_COL + cindex[:, None]) * TPD + (local_b % TPD)[None, :]
    usable = (grow <= gcol).astype(jnp.int32)
    eligible = jnp.sum(usable, axis=1)
    keys = jax.random.split(jax.random.fold_in(key, 7), DEVICES)
    perms = jax.vmap(lambda k: jax.random.permutation(k, positions))(keys).astype(jnp.int32)
    usable_perm = jnp.take_along_axis(usable, perms, axis=1)
    order = jnp.argsort(1 - usable_perm, axis=1, stable=True)
    chosen = jnp.take_along_axis(perms, order, axis=1)[:, :MAXT]
    weights = jax.random.randint(jax.random.fold_in(key, 11), (DEVICES,), 768, 1025, dtype=jnp.int32)
    counts = jnp.minimum(MAXT, eligible * weights // 1024).astype(jnp.int32)
    return ((chosen // cols_blk).astype(jnp.int32), (chosen % cols_blk).astype(jnp.int32), counts)


def draw_tile_rows(key, part):
    rows, cols, counts = tile_layout(key)
    return rows.reshape(-1)


def draw_tile_cols(key, part):
    rows, cols, counts = tile_layout(key)
    return cols.reshape(-1)


def draw_tile_count(key, part):
    rows, cols, counts = tile_layout(key)
    return counts


def shard_levels(stream_key, shape, pieces, low, largest):
    gain, own = 1.0, jax.random.fold_in(stream_key, 6)
    for axis_at, parts in pieces:
        heights = jnp.exp(jax.random.uniform(jax.random.fold_in(own, axis_at), (parts,), jnp.float32, low / len(pieces), largest / len(pieces)))
        gain = gain * jnp.repeat(heights, shape[axis_at] // parts).reshape([-1 if axis == axis_at else 1 for axis in range(len(shape))])
    return gain


def scatter_about(own_key, shape, scale, bound, cuts=(), held_as=jnp.bfloat16):
    array = jax.random.normal(own_key, shape, jnp.float32) * scale
    if len(cuts) > 0:
        array = shard_levels(own_key, shape, cuts, -0.22, 0.18) * array
    return jnp.clip(array, min=-bound, max=bound).astype(held_as)


def setup_inputs(seed: int = 0) -> dict:
    streams_of = jax.random.split(jax.random.key(seed), 6)
    x_tiles = scatter_about(streams_of[0], (NT, TILE * VECS), 1.0, 6.0, ((0, 128),), jnp.float32)
    ham_tiles = scatter_about(streams_of[1], (DEVICES * MAXT, TILE * TILE), (TILE * NT // 2) ** -0.5, 0.0625, ((0, 128),), jnp.float32)
    tile_rows = draw_tile_rows(jax.random.fold_in(streams_of[5], 71), 0)
    tile_cols = draw_tile_cols(jax.random.fold_in(streams_of[5], 71), 0)
    tile_count = draw_tile_count(jax.random.fold_in(streams_of[5], 71), 0)
    return dict(x_tiles=x_tiles, ham_tiles=ham_tiles, tile_rows=tile_rows, tile_cols=tile_cols, tile_count=tile_count)


def reference(x_tiles, ham_tiles, tile_rows, tile_cols, tile_count):
    slots = MAXT
    tiles_all = ham_tiles.reshape(DEVICES, slots, TILE, TILE)
    rows_all = tile_rows.reshape(DEVICES, slots)
    cols_all = tile_cols.reshape(DEVICES, slots)
    device_ids = jnp.arange(DEVICES, dtype=jnp.int32)

    def one_device(total, inputs):
        tiles, rows, cols, count, dev = inputs
        rindex = dev // N_COL
        cindex = dev % N_COL
        grow = (rindex * N_COL * TPD + rows).astype(jnp.int32)
        gcol = (((cols // TPD) * N_COL + cindex) * TPD + cols % TPD).astype(jnp.int32)
        live = (jnp.arange(slots) < count).astype(jnp.float32)
        far = x_tiles[gcol].reshape(slots, TILE, VECS)
        near = x_tiles[grow].reshape(slots, TILE, VECS)
        forward = jnp.einsum("sij,sjk->sik", tiles, far, precision=lax.Precision.HIGHEST)
        backward = jnp.einsum("sji,sjk->sik", tiles, near, precision=lax.Precision.HIGHEST)
        forward = forward.reshape(slots, TILE * VECS) * live[:, None]
        backward = backward.reshape(slots, TILE * VECS) * live[:, None]
        total = total.at[grow].add(forward)
        total = total.at[gcol].add(backward)
        return total, None

    start = jnp.zeros((NT, TILE * VECS), jnp.float32)
    total, _ = lax.scan(one_device, start, (tiles_all, rows_all, cols_all, tile_count, device_ids))
    return total
```

```python
import functools

import jax
import jax.numpy as jnp
from jax import lax
from jax.experimental import pallas as pl
from jax.experimental.pallas import tpu as pltpu
from jax.sharding import PartitionSpec as P

TILE = 64
VECS = 64
LANES = 2 * VECS
PAIRS = TILE // 2


F32 = jnp.float32
BF16 = jnp.bfloat16


def split(value):
    high = value.astype(BF16)
    return high, (value - high.astype(F32)).astype(BF16)


def assemble_kernel(n_rows, n_cols, key_ref, ham_ref, high_ref, low_ref, pick_ref):
    @pl.when(pl.program_id(0) == 0)
    def _():
        spots = lax.broadcasted_iota(jnp.int32, pick_ref.shape, 0)
        pick_ref[...] = jnp.where(spots == key_ref[...], 1.0, 0.0).astype(BF16)

    high, low = split(ham_ref[...])
    picks = pick_ref[...]
    for part, out_ref in ((high, high_ref), (low, low_ref)):
        dense = jnp.dot(picks, part, preferred_element_type=F32).astype(BF16)
        for q in range(ham_ref.shape[1] // LANES):
            for b in range(n_cols):
                out_ref[q * n_rows : (q + 1) * n_rows, b * LANES : (b + 1) * LANES] = dense[
                    b * n_rows : (b + 1) * n_rows, q * LANES : (q + 1) * LANES
                ]


def assemble(ham, key, n_rows, n_cols):
    slots, width = ham.shape
    step = 512
    dense = jax.ShapeDtypeStruct((PAIRS * n_rows, n_cols * LANES), BF16)
    out_spec = pl.BlockSpec((step // LANES * n_rows, n_cols * LANES), lambda i: (i, 0))
    return pl.pallas_call(
        functools.partial(assemble_kernel, n_rows, n_cols),
        grid=(width // step,),
        in_specs=[
            pl.BlockSpec((1, slots), lambda i: (0, 0)),
            pl.BlockSpec((slots, step), lambda i: (0, i)),
        ],
        out_specs=[out_spec, out_spec],
        out_shape=[dense, dense],
        scratch_shapes=[pltpu.VMEM((n_rows * n_cols, slots), BF16)],
        compiler_params=pltpu.CompilerParams(vmem_limit_bytes=24 << 20),
        cost_estimate=pl.CostEstimate(
            flops=4 * n_rows * n_cols * slots * width, bytes_accessed=12 << 20, transcendentals=0
        ),
        name="assemble",
    )(key, ham)


def backward_kernel(n_rows, near_ref, high_ref, low_ref, out_ref, turned_ref, lhs_ref):
    @pl.when(pl.program_id(0) == 0)
    def _():
        for a in range(n_rows):
            turned_ref[pl.ds(a, PAIRS, stride=n_rows), :] = near_ref[
                a // 2, (a % 2) * PAIRS : (a % 2 + 1) * PAIRS, :
            ]
        high, low = split(turned_ref[...].T)
        lhs_ref[:LANES, :] = high
        lhs_ref[LANES:, :] = low

    first = jnp.dot(lhs_ref[...], high_ref[...], preferred_element_type=F32)
    second = jnp.dot(lhs_ref[:LANES, :], low_ref[...], preferred_element_type=F32)
    total = first[:LANES] + first[LANES:] + second
    left = lax.broadcasted_iota(jnp.int32, (TILE, LANES), 1) < TILE
    for m in range(out_ref.shape[0]):
        even = total[:, (2 * m) * LANES : (2 * m + 1) * LANES]
        odd = total[:, (2 * m + 1) * LANES : (2 * m + 2) * LANES]
        out_ref[m] = jnp.where(
            left,
            even[:VECS] + pltpu.roll(even[VECS:], TILE, 1),
            pltpu.roll(odd[:VECS], TILE, 1) + odd[VECS:],
        )


def backward(near, high, low, n_rows, n_cols):
    per = 2
    wide = pl.BlockSpec((PAIRS * n_rows, per * 2 * LANES), lambda i: (0, i))
    return pl.pallas_call(
        functools.partial(backward_kernel, n_rows),
        grid=(n_cols // 2 // per,),
        in_specs=[pl.BlockSpec(near.shape, lambda i: (0, 0, 0)), wide, wide],
        out_specs=pl.BlockSpec((per, VECS, LANES), lambda i: (i, 0, 0)),
        out_shape=jax.ShapeDtypeStruct((n_cols // 2, VECS, LANES), F32),
        scratch_shapes=[
            pltpu.VMEM((PAIRS * n_rows, LANES), F32),
            pltpu.VMEM((2 * LANES, PAIRS * n_rows), BF16),
        ],
        compiler_params=pltpu.CompilerParams(vmem_limit_bytes=24 << 20),
        cost_estimate=pl.CostEstimate(
            flops=6 * LANES * high.size, bytes_accessed=9 << 20, transcendentals=0
        ),
        name="backward",
    )(near, high, low)


def forward_kernel(n_rows, n_cols, far_ref, high_ref, low_ref, out_ref, spread_ref, rhs_ref, sum_ref):
    k = pl.program_id(0)
    per = high_ref.shape[1] // LANES
    left = lax.broadcasted_iota(jnp.int32, (PAIRS, LANES), 1) < TILE
    for i in range(per):
        chunk = far_ref[i // 2, (i % 2) * PAIRS : (i % 2 + 1) * PAIRS, :]
        moved = pltpu.roll(chunk, TILE, 1)
        at = i * LANES
        zero = jnp.zeros_like(chunk)
        spread_ref[pl.ds(at, PAIRS, stride=2), :] = jnp.where(left, chunk, zero)
        spread_ref[pl.ds(at + 1, PAIRS, stride=2), :] = jnp.where(left, moved, zero)
        spread_ref[pl.ds(at + TILE, PAIRS, stride=2), :] = jnp.where(left, zero, moved)
        spread_ref[pl.ds(at + TILE + 1, PAIRS, stride=2), :] = jnp.where(left, zero, chunk)
    high, low = split(spread_ref[...])
    rhs_ref[:, :LANES] = high
    rhs_ref[:, LANES:] = low
    first = jnp.dot(high_ref[...], rhs_ref[...], preferred_element_type=F32)
    second = jnp.dot(low_ref[...], rhs_ref[:, :LANES], preferred_element_type=F32)
    total = first[:, :LANES] + first[:, LANES:] + second

    @pl.when(k == 0)
    def _():
        sum_ref[...] = total

    @pl.when(k > 0)
    def _():
        sum_ref[...] += total

    @pl.when(k == pl.num_programs(0) - 1)
    def _():
        for a in range(n_rows):
            out_ref[a // 2, (a % 2) * PAIRS : (a % 2 + 1) * PAIRS, :] = sum_ref[
                pl.ds(a, PAIRS, stride=n_rows), :
            ]


def forward(far, high, low, n_rows, n_cols):
    per = 8
    wide = pl.BlockSpec((PAIRS * n_rows, per * LANES), lambda i: (0, i))
    return pl.pallas_call(
        functools.partial(forward_kernel, n_rows, n_cols),
        grid=(n_cols // per,),
        in_specs=[
            pl.BlockSpec((per // 2, 2 * PAIRS, LANES), lambda i: (i, 0, 0)),
            wide,
            wide,
        ],
        out_specs=pl.BlockSpec((n_rows // 2, 2 * PAIRS, LANES), lambda i: (0, 0, 0)),
        out_shape=jax.ShapeDtypeStruct((n_rows // 2, 2 * PAIRS, LANES), F32),
        scratch_shapes=[
            pltpu.VMEM((per * LANES, LANES), F32),
            pltpu.VMEM((per * LANES, 2 * LANES), BF16),
            pltpu.VMEM((PAIRS * n_rows, LANES), F32),
        ],
        compiler_params=pltpu.CompilerParams(vmem_limit_bytes=24 << 20),
        cost_estimate=pl.CostEstimate(
            flops=6 * LANES * high.size, bytes_accessed=9 << 20, transcendentals=0
        ),
        name="forward",
    )(far, high, low)


def finish_kernel(upper_ref, lower_ref, out_ref, turned_ref, sum_ref):
    lower = lower_ref[0]
    for r in range(1, lower_ref.shape[0]):
        lower = lower + lower_ref[r]
    upper = upper_ref[0]
    for c in range(1, upper_ref.shape[0]):
        upper = upper + upper_ref[c]
    turned_ref[:, :VECS] = lower.T
    even = turned_ref[pl.ds(0, 2 * PAIRS, stride=2), :]
    odd = turned_ref[pl.ds(1, 2 * PAIRS, stride=2), :]
    left = lax.broadcasted_iota(jnp.int32, upper.shape, 1) < VECS
    sum_ref[...] = upper + jnp.where(left, even, pltpu.roll(odd, VECS, 1))
    for q in range(PAIRS):
        out_ref[:, q * LANES : (q + 1) * LANES] = sum_ref[pl.ds(q, 2, stride=PAIRS), :]


def finish(upper, lower):
    return pl.pallas_call(
        finish_kernel,
        out_shape=jax.ShapeDtypeStruct((2, PAIRS * LANES), F32),
        scratch_shapes=[pltpu.VMEM((LANES, LANES), F32), pltpu.VMEM((2 * PAIRS, LANES), F32)],
        compiler_params=pltpu.CompilerParams(vmem_limit_bytes=24 << 20),
        name="finish",
    )(upper, lower)


def exchange(parts, axis):
    return lax.all_to_all(parts, axis, 0, 0)


def shards(x_tiles, ham_tiles, tile_rows, tile_cols, tile_count):
    n_rows = lax.axis_size("col") * 2
    n_cols = lax.axis_size("row") * 2
    slots = ham_tiles.shape[0]
    own = x_tiles.reshape(2 * PAIRS, LANES)
    near = exchange(jnp.broadcast_to(own, (n_rows // 2,) + own.shape), "col")
    far = exchange(jnp.broadcast_to(own, (n_cols // 2,) + own.shape), "row")
    live = jnp.arange(slots) < tile_count[0]
    key = jnp.where(live, tile_cols * n_rows + tile_rows, -1)[None, :]
    high, low = assemble(ham_tiles, key, n_rows, n_cols)
    lower = exchange(backward(near, high, low, n_rows, n_cols), "row")
    upper = exchange(forward(far, high, low, n_rows, n_cols), "col")
    return finish(upper, lower)


def solution(mesh):
    placed = (
        P(("row", "col"), None),
        P(("row", "col"), None),
        P(("row", "col")),
        P(("row", "col")),
        P(("row", "col")),
    )
    return jax.shard_map(
        shards, mesh=mesh, in_specs=placed, out_specs=P(("row", "col"), None), check_vma=False
    )
```

```python
import functools

import jax
import jax.numpy as jnp
from jax import lax
from jax.experimental import pallas as pl
from jax.experimental.pallas import tpu as pltpu
from jax.sharding import PartitionSpec as P

TILE = 64
VECS = 64
LANES = 2 * VECS
PAIRS = TILE // 2


F32 = jnp.float32
BF16 = jnp.bfloat16


def split(value):
    high = value.astype(BF16)
    return high, (value - high.astype(F32)).astype(BF16)


def order(value):
    return value ^ ((value & 4) >> 1)


def assemble_kernel(n_rows, n_cols, want_low, count_ref, rows_ref, cols_ref, ham_ref, out_ref, pick_ref):
    slots = rows_ref.shape[1]
    live = lax.broadcasted_iota(jnp.int32, (1, slots), 1) < count_ref[0]
    row_owner = (rows_ref[...] >> 1) ^ lax.axis_index("col")
    col_owner = (cols_ref[...] >> 1) ^ lax.axis_index("row")
    a_at = order(row_owner) * 2 + (rows_ref[...] & 1)
    b_at = (order(col_owner >> 1) + (col_owner & 1) * (n_cols // 4)) * 2 + (cols_ref[...] & 1)
    key = jnp.where(live, b_at * n_rows + a_at, -1)
    spots = lax.broadcasted_iota(jnp.int32, pick_ref.shape, 0)
    pick_ref[...] = jnp.where(spots == key, 1.0, 0.0).astype(BF16)
    step = 512

    @pl.loop(0, ham_ref.shape[1] // step)
    def _(i):
        part = ham_ref[:, pl.ds(pl.multiple_of(i * step, step), step)]
        part = split(part)[1] if want_low else part.astype(BF16)
        dense = jnp.dot(pick_ref[...], part, preferred_element_type=F32).astype(BF16)
        for q in range(step // LANES):
            at = pl.multiple_of((i * (step // LANES) + q) * n_rows, n_rows)
            for b in range(n_cols):
                out_ref[pl.ds(at, n_rows), b * LANES : (b + 1) * LANES] = dense[
                    b * n_rows : (b + 1) * n_rows, q * LANES : (q + 1) * LANES
                ]


VMEM = pl.BlockSpec(memory_space=pltpu.VMEM)
PARAMS = pltpu.CompilerParams(vmem_limit_bytes=16 << 20)


def assemble(ham, rows, cols, count, n_rows, n_cols, want_low):
    slots, width = ham.shape
    return pl.pallas_call(
        functools.partial(assemble_kernel, n_rows, n_cols, want_low),
        in_specs=[pl.BlockSpec(memory_space=pltpu.SMEM), VMEM, VMEM, VMEM],
        out_specs=VMEM,
        out_shape=jax.ShapeDtypeStruct((PAIRS * n_rows, n_cols * LANES), BF16),
        scratch_shapes=[pltpu.VMEM((n_rows * n_cols, slots), BF16)],
        compiler_params=PARAMS,
        cost_estimate=pl.CostEstimate(
            flops=2 * n_rows * n_cols * slots * width, bytes_accessed=6 << 20, transcendentals=0
        ),
        name="assemble_low" if want_low else "assemble_high",
    )(count, rows[None, :], cols[None, :], ham)


def backward_kernel(n_rows, near0_ref, near1_ref, high_ref, low_ref, keep_ref, send_ref, turned_ref, lhs_ref):
    half = near0_ref.shape[0]
    for a in range(n_rows):
        part = near0_ref if a // 2 < half else near1_ref
        turned_ref[pl.ds(a, PAIRS, stride=n_rows), :] = part[
            a // 2 % half, (a % 2) * PAIRS : (a % 2 + 1) * PAIRS, :
        ]
    high, low = split(turned_ref[...].T)
    lhs_ref[:LANES, :] = high
    lhs_ref[LANES:, :] = low
    per = 2
    wide = per * 2 * LANES
    kept = keep_ref.shape[0]

    for start, out_ref in ((kept, send_ref), (0, keep_ref)):

        @pl.loop(0, kept // per)
        def _(i):
            at = pl.ds(pl.multiple_of((i + start // per) * wide, wide), wide)
            first = jnp.dot(lhs_ref[...], high_ref[:, at], preferred_element_type=F32)
            second = jnp.dot(lhs_ref[:LANES, :], low_ref[:, at], preferred_element_type=F32)
            total = first[:LANES] + first[LANES:] + second
            left = lax.broadcasted_iota(jnp.int32, (TILE, LANES), 1) < TILE
            for m in range(per):
                even = total[:, (2 * m) * LANES : (2 * m + 1) * LANES]
                odd = total[:, (2 * m + 1) * LANES : (2 * m + 2) * LANES]
                out_ref[i * per + m] = jnp.where(
                    left,
                    even[:VECS] + pltpu.roll(even[VECS:], TILE, 1),
                    pltpu.roll(odd[:VECS], TILE, 1) + odd[VECS:],
                )


def backward(near, high, low, n_rows, n_cols):
    half = jax.ShapeDtypeStruct((n_cols // 4, VECS, LANES), F32)
    return pl.pallas_call(
        functools.partial(backward_kernel, n_rows),
        in_specs=[VMEM] * 4,
        out_specs=[VMEM] * 2,
        out_shape=[half, half],
        scratch_shapes=[
            pltpu.VMEM((PAIRS * n_rows, LANES), F32),
            pltpu.VMEM((2 * LANES, PAIRS * n_rows), BF16),
        ],
        compiler_params=PARAMS,
        cost_estimate=pl.CostEstimate(
            flops=6 * LANES * high.size, bytes_accessed=9 << 20, transcendentals=0
        ),
        name="backward",
    )(*near, high, low)


def forward_kernel(n_rows, n_cols, far0_ref, far1_ref, high_ref, low_ref, *refs):
    out_refs, (spread_ref, rhs_ref, sum_ref) = refs[:-3], refs[-3:]
    per = 8
    wide = per * LANES

    def block(far_ref, k, offset):
        left = lax.broadcasted_iota(jnp.int32, (PAIRS, LANES), 1) < TILE
        for i in range(per):
            chunk = far_ref[k * (per // 2) + i // 2, (i % 2) * PAIRS : (i % 2 + 1) * PAIRS, :]
            moved = pltpu.roll(chunk, TILE, 1)
            at = i * LANES
            zero = jnp.zeros_like(chunk)
            spread_ref[pl.ds(at, PAIRS, stride=2), :] = jnp.where(left, chunk, zero)
            spread_ref[pl.ds(at + 1, PAIRS, stride=2), :] = jnp.where(left, moved, zero)
            spread_ref[pl.ds(at + TILE, PAIRS, stride=2), :] = jnp.where(left, zero, moved)
            spread_ref[pl.ds(at + TILE + 1, PAIRS, stride=2), :] = jnp.where(left, zero, chunk)
        high, low = split(spread_ref[...])
        rhs_ref[:, :LANES] = high
        rhs_ref[:, LANES:] = low
        at = pl.ds(pl.multiple_of((k + offset) * wide, wide), wide)
        first = jnp.dot(high_ref[:, at], rhs_ref[...], preferred_element_type=F32)
        second = jnp.dot(low_ref[:, at], rhs_ref[:, :LANES], preferred_element_type=F32)
        return first[:, :LANES] + first[:, LANES:] + second

    sum_ref[...] = jnp.zeros_like(sum_ref)
    blocks = n_cols // 2 // per
    for part, far_ref in enumerate((far0_ref, far1_ref)):

        @pl.loop(0, blocks)
        def _(k):
            sum_ref[...] += block(far_ref, k, part * blocks)

    for a in range(n_rows):
        out_refs[a // 4][a // 2 % 2, (a % 2) * PAIRS : (a % 2 + 1) * PAIRS, :] = sum_ref[
            pl.ds(a, PAIRS, stride=n_rows), :
        ]


def forward(far, high, low, n_rows, n_cols):
    per = 8
    outs = n_rows // 4
    return pl.pallas_call(
        functools.partial(forward_kernel, n_rows, n_cols),
        in_specs=[VMEM] * 4,
        out_specs=[VMEM] * outs,
        out_shape=[jax.ShapeDtypeStruct((2, 2 * PAIRS, LANES), F32)] * outs,
        scratch_shapes=[
            pltpu.VMEM((per * LANES, LANES), F32),
            pltpu.VMEM((per * LANES, 2 * LANES), BF16),
            pltpu.VMEM((PAIRS * n_rows, LANES), F32),
        ],
        compiler_params=PARAMS,
        cost_estimate=pl.CostEstimate(
            flops=6 * LANES * high.size, bytes_accessed=9 << 20, transcendentals=0
        ),
        name="forward",
    )(*far, high, low)


def finish_kernel(upper0_ref, upper1_ref, lower0_ref, lower1_ref, out_ref, turned_ref, sum_ref):
    turned_ref[:, :VECS] = (lower0_ref[0] + lower1_ref[0]).T
    upper = upper0_ref[0] + upper1_ref[0]
    even = turned_ref[pl.ds(0, 2 * PAIRS, stride=2), :]
    odd = turned_ref[pl.ds(1, 2 * PAIRS, stride=2), :]
    left = lax.broadcasted_iota(jnp.int32, upper.shape, 1) < VECS
    sum_ref[...] = upper + jnp.where(left, even, pltpu.roll(odd, VECS, 1))
    for q in range(PAIRS):
        out_ref[:, q * LANES : (q + 1) * LANES] = sum_ref[pl.ds(q, 2, stride=PAIRS), :]


def finish(upper, lower):
    return pl.pallas_call(
        finish_kernel,
        in_specs=[VMEM] * 4,
        out_specs=VMEM,
        out_shape=jax.ShapeDtypeStruct((2, PAIRS * LANES), F32),
        scratch_shapes=[pltpu.VMEM((LANES, LANES), F32), pltpu.VMEM((2 * PAIRS, LANES), F32)],
        compiler_params=PARAMS,
        name="finish",
    )(*upper, *lower)


def swap(value, axis, distance):
    pairs = [(i, i ^ distance) for i in range(lax.axis_size(axis))]
    return lax.ppermute(value, axis, pairs)


def gather(own, axis, distances):
    held = own
    for distance in distances[:-1]:
        held = jnp.concatenate([held, swap(held, axis, distance)])
    return held, swap(held, axis, distances[-1])


def shards(x_tiles, ham_tiles, tile_rows, tile_cols, tile_count):
    n_rows = lax.axis_size("col") * 2
    n_cols = lax.axis_size("row") * 2
    own = x_tiles.reshape(1, 2 * PAIRS, LANES)
    near = gather(own, "col", (1, 2, 6))
    far, across = gather(own, "row", (2, 4, 12))
    far = jnp.concatenate([far, across])
    far = far, swap(far, "row", 1)
    where = (ham_tiles, tile_rows, tile_cols, tile_count, n_rows, n_cols)
    high = assemble(*where, False)
    low = assemble(*where, True)
    keep, send = backward(near, high, low, n_rows, n_cols)
    lower = keep + swap(send, "row", 1)
    parts = [swap(lower[2:4], "row", 4), swap(lower[4:6], "row", 12), swap(lower[6:8], "row", 8)]
    lower = lower[:2] + parts[0] + parts[1] + parts[2]
    lower = lower[:1], swap(lower[1:], "row", 2)
    upper = forward(far, high, low, n_rows, n_cols)
    parts = [swap(upper[1], "col", 2), swap(upper[2], "col", 6), swap(upper[3], "col", 4)]
    upper = upper[0] + parts[0] + parts[1] + parts[2]
    upper = upper[:1], swap(upper[1:], "col", 1)
    return finish(upper, lower)


def solution(mesh):
    placed = (
        P(("row", "col"), None),
        P(("row", "col"), None),
        P(("row", "col")),
        P(("row", "col")),
        P(("row", "col")),
    )
    return jax.shard_map(
        shards, mesh=mesh, in_specs=placed, out_specs=P(("row", "col"), None), check_vma=False
    )
```

```python
import functools

import jax
import jax.numpy as jnp
from jax import lax
from jax.experimental import pallas as pl
from jax.experimental.pallas import tpu as pltpu
from jax.sharding import PartitionSpec as P


TILE = 64
VECS = 64
LANES = 2 * VECS
PAIRS = TILE // 2
WIDE = 4


F32 = jnp.float32
BF16 = jnp.bfloat16


def split(value):
    high = value.astype(BF16)
    return high, (value - high.astype(F32)).astype(BF16)


def ring_slot(step, core):
    near, far = (step ^ (step >> 1)) & 1, step >> 1
    return jnp.where(core == 0, far * 2 + near, near * 2 + far)


def place(dense, n_rows, n_cols, first, out_ref):
    for q in range(dense.shape[1] // LANES):
        at = first + q * n_rows
        at = at if isinstance(at, int) else pl.multiple_of(at, n_rows)
        for b in range(n_cols):
            out_ref[b // WIDE, pl.ds(at, n_rows), b % WIDE * LANES : (b % WIDE + 1) * LANES] = dense[
                b * n_rows : (b + 1) * n_rows, q * LANES : (q + 1) * LANES
            ]


def pick(n_rows, n_cols, count, rows, cols, shape):
    live = lax.broadcasted_iota(jnp.int32, rows.shape, 1) < count
    row = lax.axis_index("row")
    core = row & 1
    row_owner = (rows >> 1) ^ lax.axis_index("col")
    col_owner = (cols >> 1) ^ row
    row_slot = ring_slot(row_owner >> 1, core) * 2 + (row_owner & 1)
    col_slot = ring_slot(col_owner >> 2, core ^ (col_owner & 1)) * 2 + ((col_owner >> 1) & 1)
    a_at = row_slot * 2 + (rows & 1)
    b_at = (col_slot + (col_owner & 1) * (n_cols // 4)) * 2 + (cols & 1)
    key = jnp.where(live, b_at * n_rows + a_at, -1)
    spots = lax.broadcasted_iota(jnp.int32, shape, 0)
    return jnp.where(spots == key, 1.0, 0.0).astype(BF16)


def high_kernel(n_rows, n_cols, count_ref, rows_ref, cols_ref, ham_ref, out_ref, pick_ref, rest_ref):
    pick_ref[...] = pick(n_rows, n_cols, count_ref[0], rows_ref[...], cols_ref[...], pick_ref.shape)
    for i in range(ham_ref.shape[1] // STEP):
        at = slice(i * STEP, (i + 1) * STEP)
        high, rest_ref[:, at] = split(ham_ref[:, at])
        dense = jnp.dot(pick_ref[...], high, preferred_element_type=F32).astype(BF16)
        place(dense, n_rows, n_cols, i * (STEP // LANES) * n_rows, out_ref)


def low_kernel(n_rows, n_cols, tiles_ref, pick_ref, out_ref):
    for i in range(tiles_ref.shape[1] // STEP):
        part = tiles_ref[:, i * STEP : (i + 1) * STEP]
        dense = jnp.dot(pick_ref[...], part, preferred_element_type=F32).astype(BF16)
        place(dense, n_rows, n_cols, i * (STEP // LANES) * n_rows, out_ref)


VMEM = pl.BlockSpec(memory_space=pltpu.VMEM)
HBM = pl.BlockSpec(memory_space=pltpu.HBM)
PARAMS = pltpu.CompilerParams(vmem_limit_bytes=16 << 20)


def block_shape(n_rows, n_cols):
    return jax.ShapeDtypeStruct((n_cols // WIDE, PAIRS * n_rows, WIDE * LANES), BF16)


STEP = 512
LAY_BYTES = 6 << 20
LAY_FLOPS = 1 << 30


def assemble(ham, rows, cols, count, n_rows, n_cols):
    slots, width = ham.shape
    tiles = jax.ShapeDtypeStruct((slots, width), BF16)
    picks = jax.ShapeDtypeStruct((n_rows * n_cols, slots), BF16)
    cost = pl.CostEstimate(
        flops=2 * n_rows * n_cols * slots * width, bytes_accessed=6 << 20, transcendentals=0
    )
    high, picks, tiles = pl.pallas_call(
        functools.partial(high_kernel, n_rows, n_cols),
        in_specs=[pl.BlockSpec(memory_space=pltpu.SMEM)] + [VMEM] * 3,
        out_specs=[VMEM] * 3,
        out_shape=[block_shape(n_rows, n_cols), picks, tiles],
        compiler_params=PARAMS,
        cost_estimate=cost,
        name="high",
    )(count, rows[None], cols[None], ham)
    low = pl.pallas_call(
        functools.partial(low_kernel, n_rows, n_cols),
        in_specs=[VMEM] * 2,
        out_specs=VMEM,
        out_shape=block_shape(n_rows, n_cols),
        compiler_params=PARAMS,
        cost_estimate=cost,
        name="low",
    )(tiles, picks)
    return high, low


def turn(near_refs, lhs_ref, turned_ref):
    half = near_refs[0].shape[0]
    n_rows = turned_ref.shape[0] // PAIRS
    for a in range(n_rows):
        turned_ref[pl.ds(a, PAIRS, stride=n_rows), :] = near_refs[a // 2 // half][
            a // 2 % half, (a % 2) * PAIRS : (a % 2 + 1) * PAIRS, :
        ]
    high, low = split(turned_ref[...].T)
    lhs_ref[:LANES, :] = high
    lhs_ref[LANES:, :] = low


def back(lhs_ref, high_ref, low_ref, out_ref, first_block):
    per = WIDE // 2

    for i in range(out_ref.shape[0] // per):
        at = first_block + i
        first = jnp.dot(lhs_ref[...], high_ref[at], preferred_element_type=F32)
        second = jnp.dot(lhs_ref[:LANES, :], low_ref[at], preferred_element_type=F32)
        total = first[:LANES] + first[LANES:] + second
        left = lax.broadcasted_iota(jnp.int32, (TILE, LANES), 1) < TILE
        for m in range(per):
            even = total[:, (2 * m) * LANES : (2 * m + 1) * LANES]
            odd = total[:, (2 * m + 1) * LANES : (2 * m + 2) * LANES]
            out_ref[i * per + m] = jnp.where(
                left,
                even[:VECS] + pltpu.roll(even[VECS:], TILE, 1),
                pltpu.roll(odd[:VECS], TILE, 1) + odd[VECS:],
            )


def backward_send_kernel(near0_ref, near1_ref, high_ref, low_ref, out_ref, lhs_ref, turned_ref):
    turn((near0_ref, near1_ref), lhs_ref, turned_ref)
    back(lhs_ref, high_ref, low_ref, out_ref, high_ref.shape[0] // 2)


def backward_keep_kernel(lhs_ref, high_ref, low_ref, out_ref):
    back(lhs_ref, high_ref, low_ref, out_ref, 0)


def backward(near, high, low, n_rows, n_cols):
    half = jax.ShapeDtypeStruct((n_cols // 4, VECS, LANES), F32)
    cost = pl.CostEstimate(flops=3 * LANES * high.size, bytes_accessed=5 << 20, transcendentals=0)
    send, lhs = pl.pallas_call(
        backward_send_kernel,
        in_specs=[VMEM] * 4,
        out_specs=[VMEM] * 2,
        out_shape=[half, jax.ShapeDtypeStruct((2 * LANES, PAIRS * n_rows), BF16)],
        scratch_shapes=[pltpu.VMEM((PAIRS * n_rows, LANES), F32)],
        compiler_params=PARAMS,
        cost_estimate=cost,
        name="backward_send",
    )(*near, high, low)
    keep = pl.pallas_call(
        backward_keep_kernel,
        in_specs=[VMEM] * 3,
        out_specs=VMEM,
        out_shape=half,
        compiler_params=PARAMS,
        cost_estimate=cost,
        name="backward_keep",
    )(lhs, high, low)
    return keep, send


def forward_kernel(n_rows, n_cols, far0_ref, far1_ref, high_ref, low_ref, *refs):
    out_refs, (spread_ref, rhs_ref, sum_ref) = refs[:-3], refs[-3:]
    left = lax.broadcasted_iota(jnp.int32, (PAIRS, LANES), 1) < TILE
    half = n_cols // 2
    total = None
    for part, far_ref in enumerate((far0_ref, far1_ref)):
        for i in range(half):
            chunk = far_ref[i // 2, (i % 2) * PAIRS : (i % 2 + 1) * PAIRS, :]
            moved = pltpu.roll(chunk, TILE, 1)
            at = (part * half + i) * LANES
            zero = jnp.zeros_like(chunk)
            spread_ref[pl.ds(at, PAIRS, stride=2), :] = jnp.where(left, chunk, zero)
            spread_ref[pl.ds(at + 1, PAIRS, stride=2), :] = jnp.where(left, moved, zero)
            spread_ref[pl.ds(at + TILE, PAIRS, stride=2), :] = jnp.where(left, zero, moved)
            spread_ref[pl.ds(at + TILE + 1, PAIRS, stride=2), :] = jnp.where(left, zero, chunk)
            block = slice(at, at + LANES)
            rhs_ref[block, :LANES], rhs_ref[block, LANES:] = split(spread_ref[block, :])
        blocks = range(part * half // WIDE, (part + 1) * half // WIDE)
        rhs = rhs_ref[part * half * LANES : (part + 1) * half * LANES, :]
        highs = jnp.concatenate([high_ref[at] for at in blocks], axis=1)
        lows = jnp.concatenate([low_ref[at] for at in blocks], axis=1)
        first = jnp.dot(highs, rhs, preferred_element_type=F32)
        second = jnp.dot(lows, rhs[:, :LANES], preferred_element_type=F32)
        value = first[:, :LANES] + first[:, LANES:] + second
        total = value if total is None else total + value
    sum_ref[...] = total
    for a in range(n_rows):
        out_refs[a // 8][a // 2 % 4, (a % 2) * PAIRS : (a % 2 + 1) * PAIRS, :] = sum_ref[
            pl.ds(a, PAIRS, stride=n_rows), :
        ]


def forward(far, high, low, n_rows, n_cols):
    outs = n_rows // 8
    return pl.pallas_call(
        functools.partial(forward_kernel, n_rows, n_cols),
        in_specs=[VMEM] * 4,
        out_specs=[VMEM] * outs,
        out_shape=[jax.ShapeDtypeStruct((4, 2 * PAIRS, LANES), F32)] * outs,
        scratch_shapes=[
            pltpu.VMEM((n_cols * LANES, LANES), F32),
            pltpu.VMEM((n_cols * LANES, 2 * LANES), BF16),
            pltpu.VMEM((PAIRS * n_rows, LANES), F32),
        ],
        compiler_params=PARAMS,
        cost_estimate=pl.CostEstimate(
            flops=6 * LANES * high.size, bytes_accessed=9 << 20, transcendentals=0
        ),
        name="forward",
    )(*far, high, low)


def sum_kernel(keep_ref, come_ref, *out_refs):
    size = out_refs[0].shape[0]
    for i in range(keep_ref.shape[0]):
        out_refs[i // size][i % size] = keep_ref[i] + come_ref[i]


def add(keep, come):
    half = jax.ShapeDtypeStruct((keep.shape[0] // 2,) + keep.shape[1:], F32)
    return pl.pallas_call(
        sum_kernel,
        in_specs=[VMEM] * 2,
        out_specs=[VMEM] * 2,
        out_shape=[half, half],
        compiler_params=PARAMS,
    )(keep, come)


def finish_kernel(n_upper, *refs):
    uppers, lowers = refs[:n_upper], refs[n_upper:-3]
    out_ref, turned_ref, sum_ref = refs[-3:]
    lower, upper = lowers[0][0], uppers[0][0]
    for ref in lowers[1:]:
        lower = lower + ref[0]
    for ref in uppers[1:]:
        upper = upper + ref[0]
    turned_ref[:, :VECS] = lower.T
    even = turned_ref[pl.ds(0, 2 * PAIRS, stride=2), :]
    odd = turned_ref[pl.ds(1, 2 * PAIRS, stride=2), :]
    left = lax.broadcasted_iota(jnp.int32, upper.shape, 1) < VECS
    sum_ref[...] = upper + jnp.where(left, even, pltpu.roll(odd, VECS, 1))
    for q in range(PAIRS):
        out_ref[:, q * LANES : (q + 1) * LANES] = sum_ref[pl.ds(q, 2, stride=PAIRS), :]


def finish(upper, lower):
    return pl.pallas_call(
        functools.partial(finish_kernel, len(upper)),
        in_specs=[VMEM] * (len(upper) + len(lower)),
        out_specs=VMEM,
        out_shape=jax.ShapeDtypeStruct((2, PAIRS * LANES), F32),
        scratch_shapes=[pltpu.VMEM((LANES, LANES), F32), pltpu.VMEM((2 * PAIRS, LANES), F32)],
        compiler_params=PARAMS,
        name="finish",
    )(*upper, *lower)


def partner(name, r, c):
    first, second = (1, 3) if r % 2 == 0 else (3, 1)
    along = {"1": first, "2": second}.get(name[-1], 1)
    kind = name.split("_")[1][0]
    if kind == "x":
        return r ^ (along << 2), c
    if kind == "y":
        return r, c ^ (along << 1)
    return {"w": (r ^ 2, c), "c": (r ^ 1, c), "z": (r, c ^ 1)}[kind]


def swap(value, name):
    rows, cols = lax.axis_size("row"), lax.axis_size("col")
    pairs = []
    for r in range(rows):
        for c in range(cols):
            to_r, to_c = partner(name, r, c)
            pairs.append((r * cols + c, to_r * cols + to_c))
    return lax.ppermute(value, ("row", "col"), pairs)


def lay_tile(tile_ref, out_ref, at):
    for q in range(PAIRS):
        out_ref[at, pl.ds(q, 2, stride=PAIRS), :] = tile_ref[:, q * LANES : (q + 1) * LANES]


def lay_own_kernel(own_ref, out_ref):
    lay_tile(own_ref, out_ref, 0)


def lay_kernel(own_ref, other_ref, out_ref):
    out_ref[0] = own_ref[0]
    lay_tile(other_ref, out_ref, 1)


def lay(kernel, *tiles):
    return pl.pallas_call(
        kernel,
        in_specs=[VMEM] * len(tiles),
        out_specs=VMEM,
        out_shape=jax.ShapeDtypeStruct((len(tiles), 2 * PAIRS, LANES), F32),
        compiler_params=PARAMS,
        cost_estimate=pl.CostEstimate(flops=LAY_FLOPS, bytes_accessed=LAY_BYTES, transcendentals=0),
    )(*tiles)


def shards(x_tiles, ham_tiles, tile_rows, tile_cols, tile_count):
    n_rows = lax.axis_size("col") * 2
    n_cols = lax.axis_size("row") * 2
    near = swap(x_tiles, "get_z")
    far = swap(x_tiles, "get_w")
    own = lay(lay_own_kernel, x_tiles)
    near = lay(lay_kernel, own, near)
    near = jnp.concatenate([near, swap(near, "get_y1")])
    near = near, swap(near, "get_y2")
    far = lay(lay_kernel, own, far)
    far = jnp.concatenate([far, swap(far, "get_x1")])
    far = jnp.concatenate([far, swap(far, "get_x2")])
    far = far, swap(far, "get_core")
    high, low = assemble(ham_tiles, tile_rows, tile_cols, tile_count, n_rows, n_cols)
    keep, send = backward(near, high, low, n_rows, n_cols)
    keep, send = add(keep, swap(send, "put_core"))
    keep, send = add(keep, swap(send, "put_x2"))
    keep, send = add(keep, swap(send, "put_x1"))
    lower = keep, swap(send, "put_w")
    keep, send = forward(far, high, low, n_rows, n_cols)
    keep, send = add(keep, swap(send, "put_y2"))
    keep, send = add(keep, swap(send, "put_y1"))
    upper = keep, swap(send, "put_z")
    return finish(upper, lower)


def solution(mesh):
    placed = (
        P(("row", "col"), None),
        P(("row", "col"), None),
        P(("row", "col")),
        P(("row", "col")),
        P(("row", "col")),
    )
    return jax.shard_map(
        shards, mesh=mesh, in_specs=placed, out_specs=P(("row", "col"), None), check_vma=False
    )
```
